1024 devices in a mesh: dp: 8 (over y), expert: 64 (over z, x), tensor: 2 (over core).
Axes of the slice: x: 4, y: 8, z: 16, core: 2. Of those that a mesh axis runs over, the one named last changes fastest.
Arguments:
- out_grad: bfloat16 [65536, 3584], P(('dp', 'expert'), 'tensor'), may hold values from -6 to 6
- routes: int32 [65536, 8], P(('dp', 'expert')), may hold values from 0 to 255, all different within a row; in each aligned block of 128 rows (0 to 127, 128 to 255, ...) at most 5 rows name the same one
- probs: float32 [65536, 8], P(('dp', 'expert')), may hold values from 0.1 to 1
- gate_pre: bfloat16 [8, 64, 320, 1024], P('dp', 'expert', None, 'tensor'), may hold values from -8 to 8
- up_pre: bfloat16 [8, 64, 320, 1024], P('dp', 'expert', None, 'tensor'), may hold values from -6 to 6
- gate_weight: bfloat16 [64, 3584, 1024], P('expert', None, 'tensor'), may hold values from -0.09375 to 0.09375
- up_weight: bfloat16 [64, 3584, 1024], P('expert', None, 'tensor'), may hold values from -0.09375 to 0.09375
- down_weight: bfloat16 [64, 1024, 3584], P('expert', 'tensor', 'dp'), may hold values from -0.1875 to 0.1875
Outputs:
- input_grad: bfloat16 [65536, 3584], P(('dp', 'expert'), 'tensor')
The draws below stay inside these ranges and needn't reach their ends.
Inputs may be any that keep to these rules, and one draw needn't show every extreme that they name: Each row names 8 different experts. In the 128 rows of one device no expert is named more than 5 times. Ids below 64 are the experts held here, expert e at index e of expert; routes to other ids leave no slot.
All inputs are finite; a program needn't handle non-finite values.
Results may differ from the reference program's by a relative error of at most 0.0072.
Values may be sent and summed in bfloat16 or wider, within the bound.
A program may use at most 64 MiB of HBM per device.

```python
import math
import jax
import jax.numpy as jnp
import numpy as np
from jax import lax

D = 3584
FF = 1024
EXPERTS_ALL = 256
TOP = 8
TOK_DEV = 128
CAP = 5
EXPERTS = 64
SLOTS = 320
TOKENS = 65536
N_DP = 8
N_EXPERT = 64
N_TENSOR = 2


def levels(own_key, dims, shards, least, high):
    def one(dim, parts):
        draws = jax.random.uniform(jax.random.fold_in(jax.random.fold_in(own_key, 6), dim), (parts,), jnp.float32, least / len(shards), high / len(shards))
        return jnp.repeat(jnp.exp(draws), dims[dim] // parts).reshape((-1,) + (1,) * (len(dims) - dim - 1))

    factor_of = one(*shards[0])
    for cut in shards[1:]:
        factor_of = factor_of * one(*cut)
    return factor_of


def routed_block(stream_key, own, number, rows, count, top, most, lean):
    sequence = jax.random.permutation(stream_key, count)
    crowded, ordinary = shares(count, rows * top, most, lean, True), shares(count, rows * top, most, lean, False)
    places = jnp.arange(count)

    def named(lengths, offset_by):
        used = int((lengths > 0).sum())
        fixed = max(1, used // 4)
        shifted = fixed + (places - fixed + offset_by * (used - fixed)) % max(1, count - fixed)
        return jnp.zeros((count,), jnp.int32).at[sequence[jnp.where(places < fixed, places, shifted)]].set(jnp.asarray(lengths, jnp.int32))

    lengths = jnp.where(number % 4 == 0, named(crowded, number // 4), named(ordinary, number - number // 4 - 1))
    mixed = jax.random.permutation(jax.random.fold_in(own, 3), count)
    source_of, receiver = mixed[0:count // 2 * 2:2], mixed[1:count // 2 * 2:2]
    margin = jnp.minimum(lengths[source_of] - 1, most - lengths[receiver]) // 2
    margin = jnp.where((source_of == sequence[0]) | (receiver == sequence[0]) | (lengths[receiver] == 0), 0, jnp.maximum(margin, 0))
    shifted = jax.random.randint(jax.random.fold_in(own, 4), (count // 2,), 0, 1 << 20) % (margin + 1)
    lengths = lengths.at[source_of].add(-shifted).at[receiver].add(shifted)
    items = jnp.searchsorted(jnp.cumsum(lengths), jnp.arange(rows * top), side="right").astype(jnp.int32)
    table = items.reshape(top, rows).T
    table = table[jax.random.permutation(jax.random.fold_in(own, 1), rows)]
    offset_by = jax.random.randint(jax.random.fold_in(own, 2), (rows, 1), 0, top)
    return jnp.take_along_axis(table, (jnp.arange(top)[None, :] + offset_by) % top, axis=1)


def shares(number_of, total, reach, skew, full):
    portions = [(1 << 20) // math.isqrt(grade ** skew) + 1 for grade in range(1, number_of + 1)]
    largest = reach if full else min(reach, max(-(-total // number_of), total * portions[0] // sum(portions)))
    least = 1 if total - largest >= number_of - 1 else 0
    counts, rest = [largest] + [least] * (number_of - 1), total - largest - least * (number_of - 1)
    while rest > 0:
        candidates = [i for i in range(1, number_of) if counts[i] < largest] or [i for i in range(1, number_of) if counts[i] < reach]
        whole, remaining = sum([portions[i] for i in candidates]), rest
        for i in candidates:
            addition = min(reach - counts[i], max(1, remaining * portions[i] // whole), rest)
            counts[i] = counts[i] + addition
            rest = rest - addition
    return np.array(counts)


def centred(stream_key, shape, scale, limit, split=(), kind=jnp.bfloat16):
    values = scale * jax.random.normal(stream_key, shape, jnp.float32)
    if split:
        values = values * levels(stream_key, shape, split, -0.22, 0.18)
    return jnp.clip(values, -limit, limit).astype(kind)


def setup_inputs(seed: int = 0) -> dict:
    streams_of = jax.random.split(jax.random.key(seed), 9)
    out_grad = centred(streams_of[0], (TOKENS, D), 1.0, 6.0, ((0, 512), (1, 2)))
    routes_keys = jax.random.split(jax.random.fold_in(streams_of[1], 1), TOKENS // TOK_DEV)
    routes_turns = jax.random.permutation(jax.random.fold_in(streams_of[1], 3), TOKENS // TOK_DEV)
    routes = jax.vmap(lambda own, number: routed_block(jax.random.fold_in(streams_of[1], 2), own, number, TOK_DEV, EXPERTS_ALL, TOP, CAP, 2))(routes_keys, routes_turns).reshape((TOKENS, TOP))
    probs = jnp.clip(jnp.exp(math.log(1.0) - 2.3025851 * jax.random.uniform(streams_of[2], (TOKENS, TOP), jnp.float32) ** levels(streams_of[2], (TOKENS, TOP), ((0, 512),), -0.2, 0.2)), 0.1, 1.0)
    gate_pre = centred(streams_of[3], (N_DP, EXPERTS, SLOTS, FF), 2.0, 8.0, ((0, 8), (1, 64), (3, 2)))
    up_pre = centred(streams_of[4], (N_DP, EXPERTS, SLOTS, FF), 1.0, 6.0, ((0, 8), (1, 64), (3, 2)))
    gate_weight = centred(streams_of[5], (EXPERTS, D, FF), D ** -0.5, 0.09375, ((0, 64), (2, 2)))
    up_weight = centred(streams_of[6], (EXPERTS, D, FF), D ** -0.5, 0.09375, ((0, 64), (2, 2)))
    down_weight = centred(streams_of[7], (EXPERTS, FF, D), FF ** -0.5, 0.1875, ((0, 64), (1, 2), (2, 8)))
    return dict(out_grad=out_grad, routes=routes, probs=probs, gate_pre=gate_pre, up_pre=up_pre, gate_weight=gate_weight, up_weight=up_weight, down_weight=down_weight)


def slot_tables(block_routes, block_probs, experts, capacity):
    expert_ids = jnp.arange(experts, dtype=jnp.int32)
    matches = block_routes[:, :, None] == expert_ids[None, None, :]
    picked = jnp.sum(matches.astype(jnp.int32), axis=1)
    weight = jnp.sum(jnp.where(matches, block_probs[:, :, None], jnp.float32(0.0)), axis=1)
    before = jnp.cumsum(picked, axis=0) - picked
    rank_ids = jnp.arange(capacity, dtype=jnp.int32)
    select = (picked.T[:, None, :] == 1) & (before.T[:, None, :] == rank_ids[None, :, None])
    slot_scale = jnp.sum(jnp.where(select, weight.T[:, None, :], jnp.float32(0.0)), axis=2)
    return select, slot_scale


def expert_backward(slot_rows, gate_saved, up_saved, gate_matrix, up_matrix, down_matrix):
    hidden_grad = lax.dot_general(slot_rows, down_matrix, (((1,), (1,)), ((), ())), preferred_element_type=jnp.float32)
    gate_act = gate_saved.astype(jnp.float32)
    up_act = up_saved.astype(jnp.float32)
    sigmoid_gate = jax.nn.sigmoid(gate_act)
    activated = gate_act * sigmoid_gate
    derivative = sigmoid_gate * (1.0 + gate_act * (1.0 - sigmoid_gate))
    gate_grad = (hidden_grad * up_act * derivative).astype(jnp.bfloat16)
    up_grad = (hidden_grad * activated).astype(jnp.bfloat16)
    half_width = FF // N_TENSOR
    running = jnp.zeros((slot_rows.shape[0], D), jnp.float32)
    for piece_index in range(N_TENSOR):
        lower = piece_index * half_width
        upper = lower + half_width
        partial_value = lax.dot_general(gate_grad[:, lower:upper], gate_matrix[:, lower:upper], (((1,), (1,)), ((), ())), preferred_element_type=jnp.float32)
        partial_value = partial_value + lax.dot_general(up_grad[:, lower:upper], up_matrix[:, lower:upper], (((1,), (1,)), ((), ())), preferred_element_type=jnp.float32)
        rounded = lax.optimization_barrier(partial_value.astype(jnp.bfloat16))
        running = running + rounded.astype(jnp.float32)
    return running.astype(jnp.bfloat16)


def reference(out_grad, routes, probs, gate_pre, up_pre, gate_weight, up_weight, down_weight):
    group_grad = out_grad.reshape(N_DP, N_EXPERT, TOK_DEV, D)
    group_routes = routes.reshape(N_DP, N_EXPERT, TOK_DEV, TOP)
    group_probs = probs.reshape(N_DP, N_EXPERT, TOK_DEV, TOP)

    def group_backward(operands):
        grads_here, routes_here, probs_here, gate_here, up_here = operands
        select, slot_scale = jax.vmap(lambda rows_r, rows_p: slot_tables(rows_r, rows_p, N_EXPERT, CAP))(routes_here, probs_here)
        select_float = select.astype(jnp.float32)
        picked_rows = jnp.einsum('secT,sTd->secd', select_float, grads_here.astype(jnp.float32))
        outgoing = (slot_scale[..., None] * picked_rows).astype(jnp.bfloat16)
        arrived = jnp.transpose(outgoing, (1, 0, 2, 3)).reshape(N_EXPERT, N_EXPERT * CAP, D)
        returned_rows = lax.map(lambda inputs: expert_backward(*inputs), (arrived, gate_here, up_here, gate_weight, up_weight, down_weight))
        returned_rows = jnp.transpose(returned_rows.reshape(N_EXPERT, N_EXPERT, CAP, D), (1, 0, 2, 3))
        combined = jnp.einsum('secT,secd->sTd', select_float, returned_rows.astype(jnp.float32))
        return combined.astype(jnp.bfloat16)

    result = lax.map(group_backward, (group_grad, group_routes, group_probs, gate_pre, up_pre))
    return result.reshape(TOKENS, D)
```

```python
import functools

import jax
import jax.numpy as jnp
from jax import lax
from jax.experimental import pallas as pl
from jax.experimental.pallas import tpu as pltpu
from jax.sharding import PartitionSpec as P

MESH = pl.DeviceIdType.MESH
CAP = 5
NX = 4
STEPS = ((0, 8, 4, 12), (2, 14, 6, 10), (3, 13, 5, 11), (1, 15, 7, 9))
BF16 = jnp.bfloat16
F32 = jnp.float32
NT = (((1,), (1,)), ((), ()))
TN = (((0,), (0,)), ((), ()))


def kernel(
    steps, nx, routes, probs, grad_hbm, gate_pre_hbm, up_pre_hbm, gate_hbm, up_hbm, down_hbm, out,
    grad, gate_pre, up_pre, gate, up, down, spread, spread_in, select, sent, arrived, other,
    rows_own, rows_other, gate_mul, up_mul, grads, half_out, half_in, own_half, back, returned,
    total, local_sem, send_sem, recv_sem, pair_sem, y_send, y_recv, half_sem, back_send, back_recv,
):
    me, y, core = lax.axis_index("expert"), lax.axis_index("dp"), lax.axis_index("tensor")
    experts, n_dp = lax.axis_size("expert"), lax.axis_size("dp")
    nz = experts // nx
    z, x = me // nx, me % nx
    chunks, per = len(steps), len(steps[0]) * nx
    tokens, width = grad.shape
    blocks = width // 128
    message = sent.shape[2]
    hidden_width = gate.shape[1]
    deep = down_hbm.shape[0]
    tile = min(256, width)
    partner = {"tensor": 1 - core}
    ahead, behind = {"dp": lax.rem(y + 1, n_dp)}, {"dp": lax.rem(y + n_dp - 1, n_dp)}

    barrier = pltpu.get_barrier_semaphore()

    def greet(k, carry):
        pl.semaphore_signal(
            barrier, inc=1, device_id={"expert": lax.rem(me + k, experts)}, device_id_type=MESH
        )
        return carry

    lax.fori_loop(1, experts, greet, 0)
    for device in (partner, ahead, behind):
        pl.semaphore_signal(barrier, inc=1, device_id=device, device_id_type=MESH)

    own_rows = pl.ds(pl.multiple_of(y * deep, deep), deep)
    loads = [
        pltpu.make_async_copy(grad_hbm, grad, local_sem.at[0]),
        pltpu.make_async_copy(down_hbm, down.at[own_rows], local_sem.at[1]),
        pltpu.make_async_copy(gate_pre_hbm, gate_pre, local_sem.at[2]),
        pltpu.make_async_copy(up_pre_hbm, up_pre, local_sem.at[3]),
        pltpu.make_async_copy(gate_hbm, gate, local_sem.at[4]),
        pltpu.make_async_copy(up_hbm, up, local_sem.at[5]),
    ]
    for load in loads:
        load.start()

    def offsets(i):
        return [(dz, dx) for dz in steps[i] for dx in range(nx)]

    def toward(dz, dx):
        return {"expert": lax.rem(z + dz, nz) * nx + lax.rem(x + dx, nx)}

    def from_(dz, dx):
        return {"expert": lax.rem(z + nz - dz, nz) * nx + lax.rem(x + nx - dx, nx)}

    shift = nx.bit_length() - 1
    order = lax.broadcasted_iota(jnp.int32, (experts, tokens), 0)
    group = order >> shift
    dz_of = jnp.zeros_like(order)
    for j, dz in enumerate([dz for chunk in steps for dz in chunk]):
        dz_of = jnp.where(group == j, dz, dz_of)
    dx_of = order & (nx - 1)
    expert_of = ((dz_of + z) & (nz - 1)) * nx + ((dx_of + x) & (nx - 1))
    picked = jnp.zeros((experts, tokens), F32)
    weight = jnp.zeros((experts, tokens), F32)
    for k in range(routes.shape[0]):
        match = routes[k : k + 1, :] == expert_of
        picked = jnp.where(match, 1.0, picked)
        weight = jnp.where(match, probs[k : k + 1, :], weight)
    earlier = lax.broadcasted_iota(jnp.int32, (tokens, tokens), 0) < lax.broadcasted_iota(
        jnp.int32, (tokens, tokens), 1
    )
    before = jnp.dot(
        picked.astype(BF16), jnp.where(earlier, 1.0, 0.0).astype(BF16), preferred_element_type=F32
    )
    rank = jnp.where(picked > 0.5, before, -1.0)
    chosen = [jnp.where(jnp.abs(rank - r) < 0.5, 1.0, 0.0) for r in range(CAP)]
    spread[...] = jnp.zeros_like(spread)

    def put(value, r, block):
        spread[pl.ds(r * blocks + block, per, stride=message), :] = value

    def pack(destination):
        destination[...] = spread[...].reshape(per, message, 128).astype(BF16)

    def unpack(source, destination):
        spread_in[...] = source[...].astype(F32).reshape(per * message, 128)
        for r in range(CAP):
            for block in range(blocks):
                destination[r * per : (r + 1) * per, block * 128 : (block + 1) * 128] = spread_in[
                    pl.ds(r * blocks + block, per, stride=message), :
                ].astype(BF16)

    def dispatch_rows(i):
        part = slice(i * per, (i + 1) * per)
        table = jnp.concatenate([c[part] for c in chosen], axis=0)
        scale = jnp.sum(
            table * jnp.concatenate([weight[part]] * CAP, axis=0), axis=1, keepdims=True
        )
        select[i] = table.astype(BF16)
        for start in range(0, width, tile):
            rows = scale * jnp.dot(
                table.astype(BF16), grad[:, start : start + tile], preferred_element_type=F32
            )
            for r in range(CAP):
                for b in range(tile // 128):
                    put(
                        rows[r * per : (r + 1) * per, b * 128 : (b + 1) * 128],
                        r,
                        start // 128 + b,
                    )
        pack(sent.at[i])

    def exchange(i, source, target, device_of, s_sem, r_sem):
        for k, (dz, dx) in enumerate(offsets(i)):
            if dz == 0 and dx == 0:
                pltpu.make_async_copy(source.at[i, k], target.at[i, k], r_sem.at[i]).start()
            else:
                pltpu.make_async_remote_copy(
                    src_ref=source.at[i, k],
                    dst_ref=target.at[i, k],
                    send_sem=s_sem.at[i],
                    recv_sem=r_sem.at[i],
                    device_id=device_of(dz, dx),
                    device_id_type=MESH,
                ).start()

    def wait_arrival(i, target, r_sem):
        pltpu.make_async_copy(target.at[i], target.at[i], r_sem.at[i]).wait()

    def wait_sent(i, source, s_sem):
        first = 1 if offsets(i)[0] == (0, 0) else 0
        ref = source.at[i, pl.ds(first, per - first)]
        pltpu.make_async_copy(ref, ref, s_sem.at[i]).wait()

    def y_block(j):
        return down.at[pl.ds(pl.multiple_of(lax.rem(j + n_dp, n_dp) * deep, deep), deep)]

    def y_copies(s):
        copies = []
        if s < n_dp // 2:
            copies.append(
                pltpu.make_async_remote_copy(
                    src_ref=y_block(y - s), dst_ref=y_block(y - s), send_sem=y_send.at[0, s],
                    recv_sem=y_recv.at[0, s], device_id=ahead, device_id_type=MESH,
                )
            )
        if s < (n_dp - 1) // 2:
            copies.append(
                pltpu.make_async_remote_copy(
                    src_ref=y_block(y + s), dst_ref=y_block(y + s), send_sem=y_send.at[1, s],
                    recv_sem=y_recv.at[1, s], device_id=behind, device_id_type=MESH,
                )
            )
        return copies

    def y_wait(s):
        if s < n_dp // 2:
            pltpu.make_async_copy(
                y_block(y - 1 - s), y_block(y - 1 - s), y_recv.at[0, s]
            ).wait()
        if s < (n_dp - 1) // 2:
            pltpu.make_async_copy(
                y_block(y + 1 + s), y_block(y + 1 + s), y_recv.at[1, s]
            ).wait()

    def y_step(s):
        if s < n_dp // 2:
            y_wait(s)
            for copy in y_copies(s + 1):
                copy.start()

    def pair_copy(i):
        return pltpu.make_async_remote_copy(
            src_ref=arrived.at[i], dst_ref=other.at[i], send_sem=pair_sem.at[0, i],
            recv_sem=pair_sem.at[1, i], device_id=partner, device_id_type=MESH,
        )

    def half_copy(i):
        return pltpu.make_async_remote_copy(
            src_ref=half_out.at[i], dst_ref=half_in.at[i], send_sem=half_sem.at[0, i],
            recv_sem=half_sem.at[1, i], device_id=partner, device_id_type=MESH,
        )

    def factors(i):
        row = lax.broadcasted_iota(jnp.int32, (CAP * per, 1), 0)
        r_of = jnp.zeros_like(row)
        for r in range(1, CAP):
            r_of = jnp.where(row >= r * per, r, r_of)
        k_of = row - r_of * per
        dz_row = jnp.zeros_like(row)
        for j, dz in enumerate(steps[i]):
            dz_row = jnp.where((k_of >> shift) == j, dz, dz_row)
        source = ((z + nz - dz_row) & (nz - 1)) * nx + ((x + nx - (k_of & (nx - 1))) & (nx - 1))
        place = jnp.where(
            lax.broadcasted_iota(jnp.int32, (CAP * per, experts * CAP), 1) == source * CAP + r_of,
            1.0,
            0.0,
        ).astype(BF16)
        a = jnp.dot(place, gate_pre[...], preferred_element_type=F32)
        b = jnp.dot(place, up_pre[...], preferred_element_type=F32)
        q = jax.nn.sigmoid(a)
        gate_mul[i] = b * (q * (1.0 + a * (1.0 - q)))
        up_mul[i] = a * q

    def take(i):
        wait_arrival(i, arrived, recv_sem)
        pair_copy(i).start()
        unpack(arrived.at[i], rows_own.at[i])

    def half_rows(half, start):
        return pl.ds(pl.multiple_of(half * width + start, tile), tile)

    def partial(half, start):
        rows = half_rows(half, start)
        return lax.dot_general(
            grads[0], gate[rows, :], NT, preferred_element_type=F32
        ) + lax.dot_general(grads[1], up[rows, :], NT, preferred_element_type=F32)

    def work(i):
        pair_copy(i).wait()
        unpack(other.at[i], rows_other)
        own_down = down[pl.ds(pl.multiple_of(core * width, width), width), :]
        other_down = down[pl.ds(pl.multiple_of((1 - core) * width, width), width), :]
        hidden = jnp.dot(rows_own[i], own_down, preferred_element_type=F32) + jnp.dot(
            rows_other[...], other_down, preferred_element_type=F32
        )
        grads[0] = (hidden * gate_mul[i]).astype(BF16)
        grads[1] = (hidden * up_mul[i]).astype(BF16)
        for start in range(0, width, tile):
            half_out[i, :, start : start + tile] = partial(1 - core, start).astype(BF16)
        half_copy(i).start()
        for start in range(0, width, tile):
            own_half[:, start : start + tile] = partial(core, start).astype(BF16)
        half_copy(i).wait()
        for r in range(CAP):
            for block in range(blocks):
                at = (slice(r * per, (r + 1) * per), slice(block * 128, (block + 1) * 128))
                put(own_half[at].astype(F32) + half_in[(i,) + at].astype(F32), r, block)
        pack(back.at[i])
        exchange(i, back, returned, from_, back_send, back_recv)

    def gather(i):
        wait_arrival(i, returned, back_recv)
        unpack(returned.at[i], rows_other)
        for start in range(0, width, tile):
            cols = slice(start, start + tile)
            value = lax.dot_general(select[i], rows_other[:, cols], TN, preferred_element_type=F32)
            if i > 0:
                value = value + total[:, cols]
            if i == chunks - 1:
                out[:, cols] = value.astype(BF16)
            else:
                total[:, cols] = value

    loads[0].wait()
    dispatch_rows(0)
    pl.semaphore_wait(barrier, experts + 2)
    exchange(0, sent, arrived, toward, send_sem, recv_sem)
    loads[1].wait()
    for copy in y_copies(0):
        copy.start()
    for i in range(1, chunks):
        dispatch_rows(i)
        exchange(i, sent, arrived, toward, send_sem, recv_sem)
    loads[2].wait()
    loads[3].wait()
    for i in range(chunks):
        factors(i)
    loads[4].wait()
    loads[5].wait()
    y_step(0)
    take(0)
    y_step(1)
    if chunks > 1:
        take(1)
    for s in range(2, n_dp // 2):
        y_step(s)
    work(0)
    if chunks > 1:
        work(1)
    for i in range(2, chunks):
        take(i)
        work(i)
    for i in range(chunks):
        gather(i)
    for i in range(chunks):
        wait_sent(i, sent, send_sem)
        wait_sent(i, back, back_send)
    for s in range(n_dp // 2):
        for copy in y_copies(s):
            copy.wait_send()


def local(steps, nx, out_grad, routes, probs, gate_pre, up_pre, gate, up, down):
    tokens, width = out_grad.shape
    slots, hidden = gate_pre.shape[2:]
    full = gate.shape[1]
    chunks, per = len(steps), len(steps[0]) * nx
    message = -(-CAP * (width // 128) // 8) * 8
    n_dp = lax.axis_size("dp")
    experts = lax.axis_size("expert")
    flight = pltpu.VMEM((chunks, per, message, 128), BF16)
    rows = CAP * per
    dma = pltpu.SemaphoreType.DMA
    anywhere = pl.BlockSpec(memory_space=pl.ANY)
    vmem = pl.BlockSpec(memory_space=pltpu.VMEM)
    return pl.pallas_call(
        functools.partial(kernel, steps, nx),
        out_shape=jax.ShapeDtypeStruct((tokens, width), BF16),
        in_specs=[vmem] * 2 + [anywhere] * 6,
        out_specs=vmem,
        scratch_shapes=[
            pltpu.VMEM((tokens, width), BF16),
            pltpu.VMEM((slots, hidden), BF16),
            pltpu.VMEM((slots, hidden), BF16),
            pltpu.VMEM((full, hidden), BF16),
            pltpu.VMEM((full, hidden), BF16),
            pltpu.VMEM((full, hidden), BF16),
            pltpu.VMEM((per * message, 128), F32),
            pltpu.VMEM((per * message, 128), F32),
            pltpu.VMEM((chunks, rows, tokens), BF16),
            flight,
            flight,
            flight,
            pltpu.VMEM((chunks, rows, width), BF16),
            pltpu.VMEM((rows, width), BF16),
            pltpu.VMEM((chunks, rows, hidden), F32),
            pltpu.VMEM((chunks, rows, hidden), F32),
            pltpu.VMEM((2, rows, hidden), BF16),
            pltpu.VMEM((chunks, rows, width), BF16),
            pltpu.VMEM((chunks, rows, width), BF16),
            pltpu.VMEM((rows, width), BF16),
            flight,
            flight,
            pltpu.VMEM((tokens, width), F32),
            dma((6,)),
            dma((chunks,)),
            dma((chunks,)),
            dma((2, chunks)),
            dma((2, n_dp // 2)),
            dma((2, n_dp // 2)),
            dma((2, chunks)),
            dma((chunks,)),
            dma((chunks,)),
        ],
        compiler_params=pltpu.CompilerParams(
            collective_id=0, has_side_effects=True, vmem_limit_bytes=60 * 1024 * 1024
        ),
    )(
        routes.T, probs.T, out_grad, gate_pre[0, 0], up_pre[0, 0], gate[0], up[0], down[0].T
    )


def solution(mesh):
    placed = (
        P(("dp", "expert"), "tensor"),
        P(("dp", "expert"), None),
        P(("dp", "expert"), None),
        P("dp", "expert", None, "tensor"),
        P("dp", "expert", None, "tensor"),
        P("expert", None, "tensor"),
        P("expert", None, "tensor"),
        P("expert", "tensor", "dp"),
    )
    return jax.shard_map(
        functools.partial(local, STEPS, NX),
        mesh=mesh,
        in_specs=placed,
        out_specs=P(("dp", "expert"), "tensor"),
        check_vma=False,
    )
```

```python
import functools

import jax
import jax.numpy as jnp
from jax import lax
from jax.experimental import pallas as pl
from jax.experimental.pallas import tpu as pltpu
from jax.sharding import PartitionSpec as P

MESH = pl.DeviceIdType.MESH
CAP = 5
NX = 4
STEPS = ((0, 8, 9, 7), (10, 6, 11, 5), (12, 4, 13, 3), (14, 2, 15, 1))
BF16 = jnp.bfloat16
F32 = jnp.float32
NT = (((1,), (1,)), ((), ()))
TN = (((0,), (0,)), ((), ()))


def kernel(
    steps, nx, routes, probs, grad_hbm, gate_pre_hbm, up_pre_hbm, gate_hbm, up_hbm, down_hbm, out,
    grad, gate_pre, up_pre, gate, up, down, spread, spread_in, select, sent, arrived, other,
    rows_own, rows_other, gate_mul, up_mul, grads, half_out, half_in, own_half, back, returned,
    total, local_sem, send_sem, recv_sem, pair_sem, y_send, y_recv, half_sem, back_send, back_recv,
):
    me, y, core = lax.axis_index("expert"), lax.axis_index("dp"), lax.axis_index("tensor")
    experts, n_dp = lax.axis_size("expert"), lax.axis_size("dp")
    nz = experts // nx
    z, x = me // nx, me % nx
    chunks, per = len(steps), len(steps[0]) * nx
    tokens, width = grad.shape
    blocks = width // 128
    message = sent.shape[2]
    hidden_width = gate.shape[1]
    deep = down_hbm.shape[0]
    tile = min(256, width)
    partner = {"tensor": 1 - core}
    ahead, behind = {"dp": lax.rem(y + 1, n_dp)}, {"dp": lax.rem(y + n_dp - 1, n_dp)}

    barrier = pltpu.get_barrier_semaphore()

    def greet(j, carry):
        k = experts // 2 + (1 - 2 * (j % 2)) * ((j + 1) // 2)
        pl.semaphore_signal(
            barrier, inc=1, device_id={"expert": lax.rem(me + k, experts)}, device_id_type=MESH
        )
        return carry

    lax.fori_loop(0, experts - 1, greet, 0)
    for device in (partner, ahead, behind):
        pl.semaphore_signal(barrier, inc=1, device_id=device, device_id_type=MESH)

    own_rows = pl.ds(pl.multiple_of(y * deep, deep), deep)
    loads = [
        pltpu.make_async_copy(grad_hbm, grad, local_sem.at[0]),
        pltpu.make_async_copy(down_hbm, down.at[own_rows], local_sem.at[1]),
        pltpu.make_async_copy(gate_pre_hbm, gate_pre, local_sem.at[2]),
        pltpu.make_async_copy(up_pre_hbm, up_pre, local_sem.at[3]),
        pltpu.make_async_copy(gate_hbm, gate, local_sem.at[4]),
        pltpu.make_async_copy(up_hbm, up, local_sem.at[5]),
    ]
    for load in loads:
        load.start()

    def offsets(i):
        return [(dz, dx) for dz in steps[i] for dx in range(nx)]

    def toward(dz, dx):
        return {"expert": lax.rem(z + dz, nz) * nx + lax.rem(x + dx, nx)}

    def from_(dz, dx):
        return {"expert": lax.rem(z + nz - dz, nz) * nx + lax.rem(x + nx - dx, nx)}

    shift = nx.bit_length() - 1
    order = lax.broadcasted_iota(jnp.int32, (experts, tokens), 0)
    group = order >> shift
    dz_of = jnp.zeros_like(order)
    for j, dz in enumerate([dz for chunk in steps for dz in chunk]):
        dz_of = jnp.where(group == j, dz, dz_of)
    dx_of = order & (nx - 1)
    expert_of = ((dz_of + z) & (nz - 1)) * nx + ((dx_of + x) & (nx - 1))
    picked = jnp.zeros((experts, tokens), F32)
    weight = jnp.zeros((experts, tokens), F32)
    for k in range(routes.shape[0]):
        match = routes[k : k + 1, :] == expert_of
        picked = jnp.where(match, 1.0, picked)
        weight = jnp.where(match, probs[k : k + 1, :], weight)
    earlier = lax.broadcasted_iota(jnp.int32, (tokens, tokens), 0) < lax.broadcasted_iota(
        jnp.int32, (tokens, tokens), 1
    )
    before = jnp.dot(
        picked.astype(BF16), jnp.where(earlier, 1.0, 0.0).astype(BF16), preferred_element_type=F32
    )
    rank = jnp.where(picked > 0.5, before, -1.0)
    chosen = [jnp.where(jnp.abs(rank - r) < 0.5, 1.0, 0.0) for r in range(CAP)]
    spread[...] = jnp.zeros_like(spread)

    def put(value, r, block):
        spread[pl.ds(r * blocks + block, per, stride=message), :] = value

    def pack(destination):
        destination[...] = spread[...].reshape(per, message, 128).astype(BF16)

    def unpack(source, destination):
        spread_in[...] = source[...].astype(F32).reshape(per * message, 128)
        for r in range(CAP):
            for block in range(blocks):
                destination[r * per : (r + 1) * per, block * 128 : (block + 1) * 128] = spread_in[
                    pl.ds(r * blocks + block, per, stride=message), :
                ].astype(BF16)

    def dispatch_rows(i):
        part = slice(i * per, (i + 1) * per)
        table = jnp.concatenate([c[part] for c in chosen], axis=0)
        scale = jnp.sum(
            table * jnp.concatenate([weight[part]] * CAP, axis=0), axis=1, keepdims=True
        )
        select[i] = table.astype(BF16)
        for start in range(0, width, tile):
            rows = scale * jnp.dot(
                table.astype(BF16), grad[:, start : start + tile], preferred_element_type=F32
            )
            for r in range(CAP):
                for b in range(tile // 128):
                    put(
                        rows[r * per : (r + 1) * per, b * 128 : (b + 1) * 128],
                        r,
                        start // 128 + b,
                    )
        pack(sent.at[i])

    def exchange(i, source, target, device_of, s_sem, r_sem):
        for k, (dz, dx) in enumerate(offsets(i)):
            if dz == 0 and dx == 0:
                pltpu.make_async_copy(source.at[i, k], target.at[i, k], r_sem.at[i]).start()
            else:
                pltpu.make_async_remote_copy(
                    src_ref=source.at[i, k],
                    dst_ref=target.at[i, k],
                    send_sem=s_sem.at[i],
                    recv_sem=r_sem.at[i],
                    device_id=device_of(dz, dx),
                    device_id_type=MESH,
                ).start()

    def wait_arrival(i, target, r_sem):
        pltpu.make_async_copy(target.at[i], target.at[i], r_sem.at[i]).wait()

    def wait_sent(i, source, s_sem):
        first = 1 if offsets(i)[0] == (0, 0) else 0
        ref = source.at[i, pl.ds(first, per - first)]
        pltpu.make_async_copy(ref, ref, s_sem.at[i]).wait()

    def y_part(j, half):
        start = lax.rem(j + n_dp, n_dp) * deep + half * (deep // 2)
        return down.at[pl.ds(pl.multiple_of(start, deep // 2), deep // 2)]

    y_steps = n_dp - 1

    def y_copies(m):
        s, half = m // 2, m % 2
        copies = []
        for way, (j, h, device) in enumerate(((y - s, half, ahead), (y + s, 1 - half, behind))):
            copies.append(
                pltpu.make_async_remote_copy(
                    src_ref=y_part(j, h), dst_ref=y_part(j, h), send_sem=y_send.at[way, m],
                    recv_sem=y_recv.at[way, m], device_id=device, device_id_type=MESH,
                )
            )
        return copies

    def y_step(m):
        s, half = m // 2, m % 2
        for way, (j, h) in enumerate(((y - 1 - s, half), (y + 1 + s, 1 - half))):
            pltpu.make_async_copy(y_part(j, h), y_part(j, h), y_recv.at[way, m]).wait()
        if m + 2 < y_steps:
            for copy in y_copies(m + 2):
                copy.start()

    def pair_copy(i):
        return pltpu.make_async_remote_copy(
            src_ref=arrived.at[i], dst_ref=other.at[i], send_sem=pair_sem.at[0, i],
            recv_sem=pair_sem.at[1, i], device_id=partner, device_id_type=MESH,
        )

    def half_copy(i):
        return pltpu.make_async_remote_copy(
            src_ref=half_out.at[i], dst_ref=half_in.at[i], send_sem=half_sem.at[0, i],
            recv_sem=half_sem.at[1, i], device_id=partner, device_id_type=MESH,
        )

    def factors(i):
        row = lax.broadcasted_iota(jnp.int32, (CAP * per, 1), 0)
        r_of = jnp.zeros_like(row)
        for r in range(1, CAP):
            r_of = jnp.where(row >= r * per, r, r_of)
        k_of = row - r_of * per
        dz_row = jnp.zeros_like(row)
        for j, dz in enumerate(steps[i]):
            dz_row = jnp.where((k_of >> shift) == j, dz, dz_row)
        source = ((z + nz - dz_row) & (nz - 1)) * nx + ((x + nx - (k_of & (nx - 1))) & (nx - 1))
        place = jnp.where(
            lax.broadcasted_iota(jnp.int32, (CAP * per, experts * CAP), 1) == source * CAP + r_of,
            1.0,
            0.0,
        ).astype(BF16)
        a = jnp.dot(place, gate_pre[...], preferred_element_type=F32)
        b = jnp.dot(place, up_pre[...], preferred_element_type=F32)
        q = jax.nn.sigmoid(a)
        gate_mul[i] = b * (q * (1.0 + a * (1.0 - q)))
        up_mul[i] = a * q

    def take(i):
        wait_arrival(i, arrived, recv_sem)
        pair_copy(i).start()
        unpack(arrived.at[i], rows_own.at[i])

    def half_rows(half, start):
        return pl.ds(pl.multiple_of(half * width + start, tile), tile)

    def partial(half, start):
        rows = half_rows(half, start)
        return lax.dot_general(
            grads[0], gate[rows, :], NT, preferred_element_type=F32
        ) + lax.dot_general(grads[1], up[rows, :], NT, preferred_element_type=F32)

    def work(i):
        pair_copy(i).wait()
        unpack(other.at[i], rows_other)
        own_down = down[pl.ds(pl.multiple_of(core * width, width), width), :]
        other_down = down[pl.ds(pl.multiple_of((1 - core) * width, width), width), :]
        hidden = jnp.dot(rows_own[i], own_down, preferred_element_type=F32) + jnp.dot(
            rows_other[...], other_down, preferred_element_type=F32
        )
        grads[0] = (hidden * gate_mul[i]).astype(BF16)
        grads[1] = (hidden * up_mul[i]).astype(BF16)
        for start in range(0, width, tile):
            half_out[i, :, start : start + tile] = partial(1 - core, start).astype(BF16)
        half_copy(i).start()
        for start in range(0, width, tile):
            own_half[:, start : start + tile] = partial(core, start).astype(BF16)
        half_copy(i).wait()
        for r in range(CAP):
            for block in range(blocks):
                at = (slice(r * per, (r + 1) * per), slice(block * 128, (block + 1) * 128))
                put(own_half[at].astype(F32) + half_in[(i,) + at].astype(F32), r, block)
        pack(back.at[i])
        exchange(i, back, returned, from_, back_send, back_recv)

    def gather(i):
        wait_arrival(i, returned, back_recv)
        unpack(returned.at[i], rows_other)
        for start in range(0, width, tile):
            cols = slice(start, start + tile)
            value = lax.dot_general(select[i], rows_other[:, cols], TN, preferred_element_type=F32)
            if i > 0:
                value = value + total[:, cols]
            if i == chunks - 1:
                out[:, cols] = value.astype(BF16)
            else:
                total[:, cols] = value

    loads[0].wait()
    dispatch_rows(0)
    pl.semaphore_wait(barrier, experts + 2)
    exchange(0, sent, arrived, toward, send_sem, recv_sem)
    loads[1].wait()
    for m in range(min(2, y_steps)):
        for copy in y_copies(m):
            copy.start()
    for i in range(1, chunks):
        dispatch_rows(i)
        exchange(i, sent, arrived, toward, send_sem, recv_sem)
    loads[2].wait()
    loads[3].wait()
    for m in range(0, min(1, y_steps)):
        y_step(m)
    for i in range(chunks):
        factors(i)
    for m in range(1, min(4, y_steps)):
        y_step(m)
    take(0)
    for m in range(4, y_steps):
        y_step(m)
    loads[4].wait()
    loads[5].wait()
    if chunks > 1:
        take(1)
    work(0)
    if chunks > 1:
        work(1)
    for i in range(2, chunks):
        take(i)
        work(i)
    for i in range(chunks):
        gather(i)
    for i in range(chunks):
        wait_sent(i, sent, send_sem)
        wait_sent(i, back, back_send)
    for m in range(y_steps):
        for copy in y_copies(m):
            copy.wait_send()


def local(steps, nx, out_grad, routes, probs, gate_pre, up_pre, gate, up, down):
    tokens, width = out_grad.shape
    slots, hidden = gate_pre.shape[2:]
    full = gate.shape[1]
    chunks, per = len(steps), len(steps[0]) * nx
    message = -(-CAP * (width // 128) // 8) * 8
    n_dp = lax.axis_size("dp")
    experts = lax.axis_size("expert")
    flight = pltpu.VMEM((chunks, per, message, 128), BF16)
    rows = CAP * per
    dma = pltpu.SemaphoreType.DMA
    anywhere = pl.BlockSpec(memory_space=pl.ANY)
    vmem = pl.BlockSpec(memory_space=pltpu.VMEM)
    return pl.pallas_call(
        functools.partial(kernel, steps, nx),
        out_shape=jax.ShapeDtypeStruct((tokens, width), BF16),
        in_specs=[vmem] * 2 + [anywhere] * 6,
        out_specs=vmem,
        scratch_shapes=[
            pltpu.VMEM((tokens, width), BF16),
            pltpu.VMEM((slots, hidden), BF16),
            pltpu.VMEM((slots, hidden), BF16),
            pltpu.VMEM((full, hidden), BF16),
            pltpu.VMEM((full, hidden), BF16),
            pltpu.VMEM((full, hidden), BF16),
            pltpu.VMEM((per * message, 128), F32),
            pltpu.VMEM((per * message, 128), F32),
            pltpu.VMEM((chunks, rows, tokens), BF16),
            flight,
            flight,
            flight,
            pltpu.VMEM((chunks, rows, width), BF16),
            pltpu.VMEM((rows, width), BF16),
            pltpu.VMEM((chunks, rows, hidden), F32),
            pltpu.VMEM((chunks, rows, hidden), F32),
            pltpu.VMEM((2, rows, hidden), BF16),
            pltpu.VMEM((chunks, rows, width), BF16),
            pltpu.VMEM((chunks, rows, width), BF16),
            pltpu.VMEM((rows, width), BF16),
            flight,
            flight,
            pltpu.VMEM((tokens, width), F32),
            dma((6,)),
            dma((chunks,)),
            dma((chunks,)),
            dma((2, chunks)),
            dma((2, n_dp - 1)),
            dma((2, n_dp - 1)),
            dma((2, chunks)),
            dma((chunks,)),
            dma((chunks,)),
        ],
        compiler_params=pltpu.CompilerParams(
            collective_id=0, has_side_effects=True, vmem_limit_bytes=60 * 1024 * 1024
        ),
    )(
        routes.T, probs.T, out_grad, gate_pre[0, 0], up_pre[0, 0], gate[0], up[0], down[0].T
    )


def solution(mesh):
    placed = (
        P(("dp", "expert"), "tensor"),
        P(("dp", "expert"), None),
        P(("dp", "expert"), None),
        P("dp", "expert", None, "tensor"),
        P("dp", "expert", None, "tensor"),
        P("expert", None, "tensor"),
        P("expert", None, "tensor"),
        P("expert", "tensor", "dp"),
    )
    return jax.shard_map(
        functools.partial(local, STEPS, NX),
        mesh=mesh,
        in_specs=placed,
        out_specs=P(("dp", "expert"), "tensor"),
        check_vma=False,
    )
```

```python
import functools

import jax
import jax.numpy as jnp
from jax import lax
from jax.experimental import pallas as pl
from jax.experimental.pallas import tpu as pltpu
from jax.sharding import PartitionSpec as P

MESH = pl.DeviceIdType.MESH
CAP = 5
NX = 4
STEPS = ((0, 8, 9, 7), (10, 6, 11, 5), (12, 4, 13, 3), (14, 2, 15, 1))
NEAR = 2
BF16 = jnp.bfloat16
F32 = jnp.float32
NT = (((1,), (1,)), ((), ()))
TN = (((0,), (0,)), ((), ()))


def kernel(
    steps, nx, routes, probs, grad_hbm, gate_pre_hbm, up_pre_hbm, gate_hbm, up_hbm, down_hbm, out,
    grad, gate_pre, up_pre, gate, up, down, spread, spread_in, select, sent, arrived, other,
    rows_own, rows_other, gate_mul, up_mul, grads, half_out, half_in, own_half, back, returned,
    total, local_sem, send_sem, recv_sem, pair_sem, y_send, y_recv, half_sem, back_send, back_recv,
    round_sem,
):
    me, y, core = lax.axis_index("expert"), lax.axis_index("dp"), lax.axis_index("tensor")
    experts, n_dp = lax.axis_size("expert"), lax.axis_size("dp")
    nz = experts // nx
    z, x = me // nx, me % nx
    chunks, per = len(steps), len(steps[0]) * nx
    tokens, width = grad.shape
    blocks = width // 128
    message = sent.shape[2]
    hidden_width = gate.shape[1]
    deep = down_hbm.shape[0]
    tile = min(256, width)
    partner = {"tensor": 1 - core}
    ahead, behind = {"dp": lax.rem(y + 1, n_dp)}, {"dp": lax.rem(y + n_dp - 1, n_dp)}

    barrier = pltpu.get_barrier_semaphore()

    def toward(dz, dx):
        return {"expert": lax.rem(z + dz, nz) * nx + lax.rem(x + dx, nx)}

    def from_(dz, dx):
        return {"expert": lax.rem(z + nz - dz, nz) * nx + lax.rem(x + nx - dx, nx)}

    near_rows = sorted({dz % nz for dz in range(-NEAR, NEAR + 1)}, key=lambda dz: -min(dz, nz - dz))
    greeted = [(dz, dx) for dz in near_rows for dx in range(nx) if (dz, dx) != (0, 0)]
    for dz, dx in greeted:
        pl.semaphore_signal(barrier, inc=1, device_id=toward(dz, dx), device_id_type=MESH)
    for device in (partner, ahead, behind):
        pl.semaphore_signal(barrier, inc=1, device_id=device, device_id_type=MESH)

    def tell(n):
        step = NEAR << n
        for dz in (step, nz - step):
            pl.semaphore_signal(
                round_sem.at[n], inc=1, device_id=toward(dz, 0), device_id_type=MESH
            )

    rounds = 0
    while NEAR << rounds < nz // 2:
        rounds += 1

    own_rows = pl.ds(pl.multiple_of(y * deep, deep), deep)
    loads = [
        pltpu.make_async_copy(grad_hbm, grad, local_sem.at[0]),
        pltpu.make_async_copy(down_hbm, down.at[own_rows], local_sem.at[1]),
        pltpu.make_async_copy(gate_pre_hbm, gate_pre, local_sem.at[2]),
        pltpu.make_async_copy(up_pre_hbm, up_pre, local_sem.at[3]),
        pltpu.make_async_copy(gate_hbm, gate, local_sem.at[4]),
        pltpu.make_async_copy(up_hbm, up, local_sem.at[5]),
    ]
    for load in loads:
        load.start()

    def offsets(i):
        return [(dz, dx) for dz in steps[i] for dx in range(nx)]

    shift = nx.bit_length() - 1
    order = lax.broadcasted_iota(jnp.int32, (experts, tokens), 0)
    group = order >> shift
    dz_of = jnp.zeros_like(order)
    for j, dz in enumerate([dz for chunk in steps for dz in chunk]):
        dz_of = jnp.where(group == j, dz, dz_of)
    dx_of = order & (nx - 1)
    expert_of = ((dz_of + z) & (nz - 1)) * nx + ((dx_of + x) & (nx - 1))
    picked = jnp.zeros((experts, tokens), F32)
    weight = jnp.zeros((experts, tokens), F32)
    for k in range(routes.shape[0]):
        match = routes[k : k + 1, :] == expert_of
        picked = jnp.where(match, 1.0, picked)
        weight = jnp.where(match, probs[k : k + 1, :], weight)
    earlier = lax.broadcasted_iota(jnp.int32, (tokens, tokens), 0) < lax.broadcasted_iota(
        jnp.int32, (tokens, tokens), 1
    )
    before = jnp.dot(
        picked.astype(BF16), jnp.where(earlier, 1.0, 0.0).astype(BF16), preferred_element_type=F32
    )
    rank = jnp.where(picked > 0.5, before, -1.0)
    chosen = [jnp.where(jnp.abs(rank - r) < 0.5, 1.0, 0.0) for r in range(CAP)]
    spread[...] = jnp.zeros_like(spread)

    def put(value, r, block):
        spread[pl.ds(r * blocks + block, per, stride=message), :] = value

    def pack(destination):
        destination[...] = spread[...].reshape(per, message, 128).astype(BF16)

    def unpack(source, destination):
        spread_in[...] = source[...].astype(F32).reshape(per * message, 128)
        for r in range(CAP):
            for block in range(blocks):
                destination[r * per : (r + 1) * per, block * 128 : (block + 1) * 128] = spread_in[
                    pl.ds(r * blocks + block, per, stride=message), :
                ].astype(BF16)

    def dispatch_rows(i):
        part = slice(i * per, (i + 1) * per)
        table = jnp.concatenate([c[part] for c in chosen], axis=0)
        scale = jnp.sum(
            table * jnp.concatenate([weight[part]] * CAP, axis=0), axis=1, keepdims=True
        )
        select[i] = table.astype(BF16)
        for start in range(0, width, tile):
            rows = scale * jnp.dot(
                table.astype(BF16), grad[:, start : start + tile], preferred_element_type=F32
            )
            for r in range(CAP):
                for b in range(tile // 128):
                    put(
                        rows[r * per : (r + 1) * per, b * 128 : (b + 1) * 128],
                        r,
                        start // 128 + b,
                    )
        pack(sent.at[i])

    def exchange(i, source, target, device_of, s_sem, r_sem):
        for k, (dz, dx) in enumerate(offsets(i)):
            if dz == 0 and dx == 0:
                pltpu.make_async_copy(source.at[i, k], target.at[i, k], r_sem.at[i]).start()
            else:
                pltpu.make_async_remote_copy(
                    src_ref=source.at[i, k],
                    dst_ref=target.at[i, k],
                    send_sem=s_sem.at[i],
                    recv_sem=r_sem.at[i],
                    device_id=device_of(dz, dx),
                    device_id_type=MESH,
                ).start()

    def wait_arrival(i, target, r_sem):
        pltpu.make_async_copy(target.at[i], target.at[i], r_sem.at[i]).wait()

    def wait_sent(i, source, s_sem):
        first = 1 if offsets(i)[0] == (0, 0) else 0
        ref = source.at[i, pl.ds(first, per - first)]
        pltpu.make_async_copy(ref, ref, s_sem.at[i]).wait()

    def y_part(j, half):
        start = lax.rem(j + n_dp, n_dp) * deep + half * (deep // 2)
        return down.at[pl.ds(pl.multiple_of(start, deep // 2), deep // 2)]

    y_steps = n_dp - 1

    def y_copies(m):
        s, half = m // 2, m % 2
        copies = []
        for way, (j, h, device) in enumerate(((y - s, half, ahead), (y + s, 1 - half, behind))):
            copies.append(
                pltpu.make_async_remote_copy(
                    src_ref=y_part(j, h), dst_ref=y_part(j, h), send_sem=y_send.at[way, m],
                    recv_sem=y_recv.at[way, m], device_id=device, device_id_type=MESH,
                )
            )
        return copies

    def y_step(m):
        s, half = m // 2, m % 2
        for way, (j, h) in enumerate(((y - 1 - s, half), (y + 1 + s, 1 - half))):
            pltpu.make_async_copy(y_part(j, h), y_part(j, h), y_recv.at[way, m]).wait()
        if m + 2 < y_steps:
            for copy in y_copies(m + 2):
                copy.start()

    def pair_copy(i):
        return pltpu.make_async_remote_copy(
            src_ref=arrived.at[i], dst_ref=other.at[i], send_sem=pair_sem.at[0, i],
            recv_sem=pair_sem.at[1, i], device_id=partner, device_id_type=MESH,
        )

    def half_copy(i):
        return pltpu.make_async_remote_copy(
            src_ref=half_out.at[i], dst_ref=half_in.at[i], send_sem=half_sem.at[0, i],
            recv_sem=half_sem.at[1, i], device_id=partner, device_id_type=MESH,
        )

    def factors(i):
        row = lax.broadcasted_iota(jnp.int32, (CAP * per, 1), 0)
        r_of = jnp.zeros_like(row)
        for r in range(1, CAP):
            r_of = jnp.where(row >= r * per, r, r_of)
        k_of = row - r_of * per
        dz_row = jnp.zeros_like(row)
        for j, dz in enumerate(steps[i]):
            dz_row = jnp.where((k_of >> shift) == j, dz, dz_row)
        source = ((z + nz - dz_row) & (nz - 1)) * nx + ((x + nx - (k_of & (nx - 1))) & (nx - 1))
        place = jnp.where(
            lax.broadcasted_iota(jnp.int32, (CAP * per, experts * CAP), 1) == source * CAP + r_of,
            1.0,
            0.0,
        ).astype(BF16)
        a = jnp.dot(place, gate_pre[...], preferred_element_type=F32)
        b = jnp.dot(place, up_pre[...], preferred_element_type=F32)
        q = jax.nn.sigmoid(a)
        gate_mul[i] = b * (q * (1.0 + a * (1.0 - q)))
        up_mul[i] = a * q

    def take(i):
        wait_arrival(i, arrived, recv_sem)
        pair_copy(i).start()
        unpack(arrived.at[i], rows_own.at[i])

    def half_rows(half, start):
        return pl.ds(pl.multiple_of(half * width + start, tile), tile)

    def partial(half, start):
        rows = half_rows(half, start)
        return lax.dot_general(
            grads[0], gate[rows, :], NT, preferred_element_type=F32
        ) + lax.dot_general(grads[1], up[rows, :], NT, preferred_element_type=F32)

    def work(i):
        pair_copy(i).wait()
        unpack(other.at[i], rows_other)
        own_down = down[pl.ds(pl.multiple_of(core * width, width), width), :]
        other_down = down[pl.ds(pl.multiple_of((1 - core) * width, width), width), :]
        hidden = jnp.dot(rows_own[i], own_down, preferred_element_type=F32) + jnp.dot(
            rows_other[...], other_down, preferred_element_type=F32
        )
        grads[0] = (hidden * gate_mul[i]).astype(BF16)
        grads[1] = (hidden * up_mul[i]).astype(BF16)
        for start in range(0, width, tile):
            half_out[i, :, start : start + tile] = partial(1 - core, start).astype(BF16)
        half_copy(i).start()
        for start in range(0, width, tile):
            own_half[:, start : start + tile] = partial(core, start).astype(BF16)
        half_copy(i).wait()
        for r in range(CAP):
            for block in range(blocks):
                at = (slice(r * per, (r + 1) * per), slice(block * 128, (block + 1) * 128))
                put(own_half[at].astype(F32) + half_in[(i,) + at].astype(F32), r, block)
        pack(back.at[i])
        exchange(i, back, returned, from_, back_send, back_recv)

    def gather(i):
        wait_arrival(i, returned, back_recv)
        unpack(returned.at[i], rows_other)
        for start in range(0, width, tile):
            cols = slice(start, start + tile)
            value = lax.dot_general(select[i], rows_other[:, cols], TN, preferred_element_type=F32)
            if i > 0:
                value = value + total[:, cols]
            if i == chunks - 1:
                out[:, cols] = value.astype(BF16)
            else:
                total[:, cols] = value

    near = chunks - 1
    loads[0].wait()
    dispatch_rows(near)
    pl.semaphore_wait(barrier, len(greeted) + 3)
    if rounds:
        tell(0)
    exchange(near, sent, arrived, toward, send_sem, recv_sem)
    loads[1].wait()
    for m in range(min(2, y_steps)):
        for copy in y_copies(m):
            copy.start()
    for n in range(1, rounds):
        pl.semaphore_wait(round_sem.at[n - 1], 2)
        tell(n)
    for i in range(near):
        dispatch_rows(i)
        if i == 0 and rounds:
            pl.semaphore_wait(round_sem.at[rounds - 1], 2)
        exchange(i, sent, arrived, toward, send_sem, recv_sem)
    loads[2].wait()
    loads[3].wait()
    for m in range(0, min(1, y_steps)):
        y_step(m)
    for i in range(chunks):
        factors(i)
    for m in range(1, min(4, y_steps)):
        y_step(m)
    take(near)
    if near > 0:
        take(0)
    for m in range(4, y_steps):
        y_step(m)
    loads[4].wait()
    loads[5].wait()
    if near > 1:
        take(1)
    for i in range(min(2, near)):
        work(i)
    for i in range(2, near):
        take(i)
        work(i)
    work(near)
    for i in range(chunks):
        gather(i)
    for i in range(chunks):
        wait_sent(i, sent, send_sem)
        wait_sent(i, back, back_send)
    for m in range(y_steps):
        for copy in y_copies(m):
            copy.wait_send()


def local(steps, nx, out_grad, routes, probs, gate_pre, up_pre, gate, up, down):
    tokens, width = out_grad.shape
    slots, hidden = gate_pre.shape[2:]
    full = gate.shape[1]
    chunks, per = len(steps), len(steps[0]) * nx
    message = -(-CAP * (width // 128) // 8) * 8
    n_dp = lax.axis_size("dp")
    experts = lax.axis_size("expert")
    flight = pltpu.VMEM((chunks, per, message, 128), BF16)
    rows = CAP * per
    dma = pltpu.SemaphoreType.DMA
    anywhere = pl.BlockSpec(memory_space=pl.ANY)
    vmem = pl.BlockSpec(memory_space=pltpu.VMEM)
    return pl.pallas_call(
        functools.partial(kernel, steps, nx),
        out_shape=jax.ShapeDtypeStruct((tokens, width), BF16),
        in_specs=[vmem] * 2 + [anywhere] * 6,
        out_specs=vmem,
        scratch_shapes=[
            pltpu.VMEM((tokens, width), BF16),
            pltpu.VMEM((slots, hidden), BF16),
            pltpu.VMEM((slots, hidden), BF16),
            pltpu.VMEM((full, hidden), BF16),
            pltpu.VMEM((full, hidden), BF16),
            pltpu.VMEM((full, hidden), BF16),
            pltpu.VMEM((per * message, 128), F32),
            pltpu.VMEM((per * message, 128), F32),
            pltpu.VMEM((chunks, rows, tokens), BF16),
            flight,
            flight,
            flight,
            pltpu.VMEM((chunks, rows, width), BF16),
            pltpu.VMEM((rows, width), BF16),
            pltpu.VMEM((chunks, rows, hidden), F32),
            pltpu.VMEM((chunks, rows, hidden), F32),
            pltpu.VMEM((2, rows, hidden), BF16),
            pltpu.VMEM((chunks, rows, width), BF16),
            pltpu.VMEM((chunks, rows, width), BF16),
            pltpu.VMEM((rows, width), BF16),
            flight,
            flight,
            pltpu.VMEM((tokens, width), F32),
            dma((6,)),
            dma((chunks,)),
            dma((chunks,)),
            dma((2, chunks)),
            dma((2, n_dp - 1)),
            dma((2, n_dp - 1)),
            dma((2, chunks)),
            dma((chunks,)),
            dma((chunks,)),
            pltpu.SemaphoreType.REGULAR((4,)),
        ],
        compiler_params=pltpu.CompilerParams(
            collective_id=0, has_side_effects=True, vmem_limit_bytes=60 * 1024 * 1024
        ),
    )(
        routes.T, probs.T, out_grad, gate_pre[0, 0], up_pre[0, 0], gate[0], up[0], down[0].T
    )


def solution(mesh):
    placed = (
        P(("dp", "expert"), "tensor"),
        P(("dp", "expert"), None),
        P(("dp", "expert"), None),
        P("dp", "expert", None, "tensor"),
        P("dp", "expert", None, "tensor"),
        P("expert", None, "tensor"),
        P("expert", None, "tensor"),
        P("expert", "tensor", "dp"),
    )
    return jax.shard_map(
        functools.partial(local, STEPS, NX),
        mesh=mesh,
        in_specs=placed,
        out_specs=P(("dp", "expert"), "tensor"),
        check_vma=False,
    )
```

```python
import functools

import jax
import jax.numpy as jnp
from jax import lax
from jax.experimental import pallas as pl
from jax.experimental.pallas import tpu as pltpu
from jax.sharding import PartitionSpec as P

MESH = pl.DeviceIdType.MESH
CAP = 5
NX = 4
STEPS = ((0, 8, 9, 7), (10, 6, 11, 5), (12, 4, 13, 3), (14, 2, 15, 1))
NEAR = 2
BF16 = jnp.bfloat16
F32 = jnp.float32
NT = (((1,), (1,)), ((), ()))


def kernel(
    steps, nx, routes, probs, grad_hbm, gate_pre_hbm, up_pre_hbm, gate_hbm, up_hbm, down_hbm, out,
    grad, gate_pre, up_pre, gate, up, down, spread, spread_in, select, sent, arrived, other,
    rows_own, rows_other, gate_mul, up_mul, grads, half_out, half_in, own_half, back, returned,
    total, local_sem, send_sem, recv_sem, pair_sem, y_send, y_recv, half_sem, back_send, back_recv,
    round_sem, select_t, combined, out_sem,
):
    me, y, core = lax.axis_index("expert"), lax.axis_index("dp"), lax.axis_index("tensor")
    experts, n_dp = lax.axis_size("expert"), lax.axis_size("dp")
    nz = experts // nx
    z, x = me // nx, me % nx
    chunks, per = len(steps), len(steps[0]) * nx
    tokens, width = grad.shape
    blocks = width // 128
    message = sent.shape[2]
    hidden_width = gate.shape[1]
    deep = down_hbm.shape[0]
    tile = min(256, width)
    partner = {"tensor": 1 - core}
    ahead, behind = {"dp": lax.rem(y + 1, n_dp)}, {"dp": lax.rem(y + n_dp - 1, n_dp)}

    barrier = pltpu.get_barrier_semaphore()

    def toward(dz, dx):
        return {"expert": lax.rem(z + dz, nz) * nx + lax.rem(x + dx, nx)}

    def from_(dz, dx):
        return {"expert": lax.rem(z + nz - dz, nz) * nx + lax.rem(x + nx - dx, nx)}

    near_rows = sorted({dz % nz for dz in range(-NEAR, NEAR + 1)}, key=lambda dz: -min(dz, nz - dz))
    greeted = [(dz, dx) for dz in near_rows for dx in range(nx) if (dz, dx) != (0, 0)]
    for dz, dx in greeted:
        pl.semaphore_signal(barrier, inc=1, device_id=toward(dz, dx), device_id_type=MESH)
    for device in (partner, ahead, behind):
        pl.semaphore_signal(barrier, inc=1, device_id=device, device_id_type=MESH)

    def tell(n):
        step = NEAR << n
        for dz in (step, nz - step):
            pl.semaphore_signal(
                round_sem.at[n], inc=1, device_id=toward(dz, 0), device_id_type=MESH
            )

    rounds = 0
    while NEAR << rounds < nz // 2:
        rounds += 1

    own_rows = pl.ds(pl.multiple_of(y * deep, deep), deep)
    loads = [
        pltpu.make_async_copy(grad_hbm, grad, local_sem.at[0]),
        pltpu.make_async_copy(down_hbm, down.at[own_rows], local_sem.at[1]),
        pltpu.make_async_copy(gate_pre_hbm, gate_pre, local_sem.at[2]),
        pltpu.make_async_copy(up_pre_hbm, up_pre, local_sem.at[3]),
        pltpu.make_async_copy(gate_hbm, gate, local_sem.at[4]),
        pltpu.make_async_copy(up_hbm, up, local_sem.at[5]),
    ]
    for load in loads:
        load.start()

    def offsets(i):
        return [(dz, dx) for dz in steps[i] for dx in range(nx)]

    shift = nx.bit_length() - 1
    order = lax.broadcasted_iota(jnp.int32, (experts, tokens), 0)
    group = order >> shift
    dz_of = jnp.zeros_like(order)
    for j, dz in enumerate([dz for chunk in steps for dz in chunk]):
        dz_of = jnp.where(group == j, dz, dz_of)
    dx_of = order & (nx - 1)
    expert_of = ((dz_of + z) & (nz - 1)) * nx + ((dx_of + x) & (nx - 1))
    picked = jnp.zeros((experts, tokens), F32)
    weight = jnp.zeros((experts, tokens), F32)
    for k in range(routes.shape[0]):
        match = routes[k : k + 1, :] == expert_of
        picked = jnp.where(match, 1.0, picked)
        weight = jnp.where(match, probs[k : k + 1, :], weight)
    earlier = lax.broadcasted_iota(jnp.int32, (tokens, tokens), 0) < lax.broadcasted_iota(
        jnp.int32, (tokens, tokens), 1
    )
    before = jnp.dot(
        picked.astype(BF16), jnp.where(earlier, 1.0, 0.0).astype(BF16), preferred_element_type=F32
    )
    rank = jnp.where(picked > 0.5, before, -1.0)
    chosen = [jnp.where(jnp.abs(rank - r) < 0.5, 1.0, 0.0) for r in range(CAP)]
    for row in range(CAP * blocks, message):
        spread[pl.ds(row, per, stride=message), :] = jnp.zeros((per, 128), F32)

    def put(value, r, block):
        spread[pl.ds(r * blocks + block, per, stride=message), :] = value

    def pack(destination):
        destination[...] = spread[...].reshape(per, message, 128).astype(BF16)

    def unpack(source, destination):
        spread_in[...] = source[...].astype(F32).reshape(per * message, 128)
        for r in range(CAP):
            for block in range(blocks):
                destination[r * per : (r + 1) * per, block * 128 : (block + 1) * 128] = spread_in[
                    pl.ds(r * blocks + block, per, stride=message), :
                ].astype(BF16)

    def dispatch_rows(i):
        part = slice(i * per, (i + 1) * per)
        table = jnp.concatenate([c[part] for c in chosen], axis=0)
        scale = jnp.sum(
            table * jnp.concatenate([weight[part]] * CAP, axis=0), axis=1, keepdims=True
        )
        select[i] = table.astype(BF16)
        for start in range(0, width, tile):
            rows = scale * jnp.dot(
                table.astype(BF16), grad[:, start : start + tile], preferred_element_type=F32
            )
            for r in range(CAP):
                for b in range(tile // 128):
                    put(
                        rows[r * per : (r + 1) * per, b * 128 : (b + 1) * 128],
                        r,
                        start // 128 + b,
                    )
        pack(sent.at[i])

    def exchange(i, source, target, device_of, s_sem, r_sem):
        for k, (dz, dx) in enumerate(offsets(i)):
            if dz == 0 and dx == 0:
                pltpu.make_async_copy(source.at[i, k], target.at[i, k], r_sem.at[i]).start()
            else:
                pltpu.make_async_remote_copy(
                    src_ref=source.at[i, k],
                    dst_ref=target.at[i, k],
                    send_sem=s_sem.at[i],
                    recv_sem=r_sem.at[i],
                    device_id=device_of(dz, dx),
                    device_id_type=MESH,
                ).start()

    def wait_arrival(i, target, r_sem):
        pltpu.make_async_copy(target.at[i], target.at[i], r_sem.at[i]).wait()

    def wait_sent(i, source, s_sem):
        first = 1 if offsets(i)[0] == (0, 0) else 0
        ref = source.at[i, pl.ds(first, per - first)]
        pltpu.make_async_copy(ref, ref, s_sem.at[i]).wait()

    def y_part(j, half):
        start = lax.rem(j + n_dp, n_dp) * deep + half * (deep // 2)
        return down.at[pl.ds(pl.multiple_of(start, deep // 2), deep // 2)]

    y_steps = n_dp - 1

    def y_copies(m):
        s, half = m // 2, m % 2
        copies = []
        for way, (j, h, device) in enumerate(((y - s, half, ahead), (y + s, 1 - half, behind))):
            copies.append(
                pltpu.make_async_remote_copy(
                    src_ref=y_part(j, h), dst_ref=y_part(j, h), send_sem=y_send.at[way, m],
                    recv_sem=y_recv.at[way, m], device_id=device, device_id_type=MESH,
                )
            )
        return copies

    def y_step(m):
        s, half = m // 2, m % 2
        for way, (j, h) in enumerate(((y - 1 - s, half), (y + 1 + s, 1 - half))):
            pltpu.make_async_copy(y_part(j, h), y_part(j, h), y_recv.at[way, m]).wait()
        if m + 2 < y_steps:
            for copy in y_copies(m + 2):
                copy.start()

    def pair_copy(i):
        return pltpu.make_async_remote_copy(
            src_ref=arrived.at[i], dst_ref=other.at[i], send_sem=pair_sem.at[0, i],
            recv_sem=pair_sem.at[1, i], device_id=partner, device_id_type=MESH,
        )

    def half_copy(i):
        return pltpu.make_async_remote_copy(
            src_ref=half_out.at[i], dst_ref=half_in.at[i], send_sem=half_sem.at[0, i],
            recv_sem=half_sem.at[1, i], device_id=partner, device_id_type=MESH,
        )

    def factors(i):
        row = lax.broadcasted_iota(jnp.int32, (CAP * per, 1), 0)
        r_of = jnp.zeros_like(row)
        for r in range(1, CAP):
            r_of = jnp.where(row >= r * per, r, r_of)
        k_of = row - r_of * per
        dz_row = jnp.zeros_like(row)
        for j, dz in enumerate(steps[i]):
            dz_row = jnp.where((k_of >> shift) == j, dz, dz_row)
        source = ((z + nz - dz_row) & (nz - 1)) * nx + ((x + nx - (k_of & (nx - 1))) & (nx - 1))
        place = jnp.where(
            lax.broadcasted_iota(jnp.int32, (CAP * per, experts * CAP), 1) == source * CAP + r_of,
            1.0,
            0.0,
        ).astype(BF16)
        a = jnp.dot(place, gate_pre[...], preferred_element_type=F32)
        b = jnp.dot(place, up_pre[...], preferred_element_type=F32)
        q = jax.nn.sigmoid(a)
        select_t[i] = jnp.transpose(select[i].astype(F32)).astype(BF16)
        gate_mul[i] = b * (q * (1.0 + a * (1.0 - q)))
        up_mul[i] = a * q

    def take(i):
        wait_arrival(i, arrived, recv_sem)
        pair_copy(i).start()
        unpack(arrived.at[i], rows_own.at[i])

    def half_rows(half, start):
        return pl.ds(pl.multiple_of(half * width + start, tile), tile)

    def partial(half, start):
        rows = half_rows(half, start)
        return lax.dot_general(
            grads[0], gate[rows, :], NT, preferred_element_type=F32
        ) + lax.dot_general(grads[1], up[rows, :], NT, preferred_element_type=F32)

    def work(i):
        pair_copy(i).wait()
        unpack(other.at[i], rows_other)
        own_down = down[pl.ds(pl.multiple_of(core * width, width), width), :]
        other_down = down[pl.ds(pl.multiple_of((1 - core) * width, width), width), :]
        hidden = jnp.dot(rows_own[i], own_down, preferred_element_type=F32) + jnp.dot(
            rows_other[...], other_down, preferred_element_type=F32
        )
        grads[0] = (hidden * gate_mul[i]).astype(BF16)
        grads[1] = (hidden * up_mul[i]).astype(BF16)
        for start in range(0, width, tile):
            half_out[i, :, start : start + tile] = partial(1 - core, start).astype(BF16)
        half_copy(i).start()
        for start in range(0, width, tile):
            own_half[:, start : start + tile] = partial(core, start).astype(BF16)
        half_copy(i).wait()
        for r in range(CAP):
            for block in range(blocks):
                at = (slice(r * per, (r + 1) * per), slice(block * 128, (block + 1) * 128))
                put(own_half[at].astype(F32) + half_in[(i,) + at].astype(F32), r, block)
        pack(back.at[i])
        exchange(i, back, returned, from_, back_send, back_recv)

    def gather(i):
        wait_arrival(i, returned, back_recv)
        unpack(returned.at[i], rows_other)
        for n, start in enumerate(range(0, width, tile)):
            cols = slice(start, start + tile)
            value = jnp.dot(select_t[i], rows_other[:, cols], preferred_element_type=F32)
            if i > 0:
                value = value + total[:, cols]
            if i == chunks - 1:
                combined[:, cols] = value.astype(BF16)
                out_copy(n).start()
            else:
                total[:, cols] = value

    def out_copy(n):
        cols = slice(n * tile, (n + 1) * tile)
        return pltpu.make_async_copy(combined.at[:, cols], out.at[:, cols], out_sem.at[n])

    near = chunks - 1
    loads[0].wait()
    dispatch_rows(near)
    pl.semaphore_wait(barrier, len(greeted) + 3)
    if rounds:
        tell(0)
    exchange(near, sent, arrived, toward, send_sem, recv_sem)
    loads[1].wait()
    for m in range(min(2, y_steps)):
        for copy in y_copies(m):
            copy.start()
    for n in range(1, rounds):
        pl.semaphore_wait(round_sem.at[n - 1], 2)
        tell(n)
    for i in range(near):
        dispatch_rows(i)
        if i == 0 and rounds:
            pl.semaphore_wait(round_sem.at[rounds - 1], 2)
        exchange(i, sent, arrived, toward, send_sem, recv_sem)
    loads[2].wait()
    loads[3].wait()
    for m in range(0, min(1, y_steps)):
        y_step(m)
    for i in range(chunks):
        factors(i)
    for m in range(1, min(4, y_steps)):
        y_step(m)
    take(near)
    if near > 0:
        take(0)
    for m in range(4, y_steps):
        y_step(m)
    loads[4].wait()
    loads[5].wait()
    if near > 1:
        take(1)
    for i in range(min(2, near)):
        work(i)
    for i in range(2, near):
        take(i)
        work(i)
    work(near)
    for i in range(chunks):
        gather(i)
    for n in range(width // tile):
        out_copy(n).wait()
    for i in range(chunks):
        wait_sent(i, sent, send_sem)
        wait_sent(i, back, back_send)
    for m in range(y_steps):
        for copy in y_copies(m):
            copy.wait_send()


def local(steps, nx, out_grad, routes, probs, gate_pre, up_pre, gate, up, down):
    tokens, width = out_grad.shape
    slots, hidden = gate_pre.shape[2:]
    full = gate.shape[1]
    chunks, per = len(steps), len(steps[0]) * nx
    message = -(-CAP * (width // 128) // 8) * 8
    n_dp = lax.axis_size("dp")
    experts = lax.axis_size("expert")
    flight = pltpu.VMEM((chunks, per, message, 128), BF16)
    rows = CAP * per
    dma = pltpu.SemaphoreType.DMA
    anywhere = pl.BlockSpec(memory_space=pl.ANY)
    vmem = pl.BlockSpec(memory_space=pltpu.VMEM)
    return pl.pallas_call(
        functools.partial(kernel, steps, nx),
        out_shape=jax.ShapeDtypeStruct((tokens, width), BF16),
        in_specs=[vmem] * 2 + [anywhere] * 6,
        out_specs=anywhere,
        scratch_shapes=[
            pltpu.VMEM((tokens, width), BF16),
            pltpu.VMEM((slots, hidden), BF16),
            pltpu.VMEM((slots, hidden), BF16),
            pltpu.VMEM((full, hidden), BF16),
            pltpu.VMEM((full, hidden), BF16),
            pltpu.VMEM((full, hidden), BF16),
            pltpu.VMEM((per * message, 128), F32),
            pltpu.VMEM((per * message, 128), F32),
            pltpu.VMEM((chunks, rows, tokens), BF16),
            flight,
            flight,
            flight,
            pltpu.VMEM((chunks, rows, width), BF16),
            pltpu.VMEM((rows, width), BF16),
            pltpu.VMEM((chunks, rows, hidden), F32),
            pltpu.VMEM((chunks, rows, hidden), F32),
            pltpu.VMEM((2, rows, hidden), BF16),
            pltpu.VMEM((chunks, rows, width), BF16),
            pltpu.VMEM((chunks, rows, width), BF16),
            pltpu.VMEM((rows, width), BF16),
            flight,
            flight,
            pltpu.VMEM((tokens, width), F32),
            dma((6,)),
            dma((chunks,)),
            dma((chunks,)),
            dma((2, chunks)),
            dma((2, n_dp - 1)),
            dma((2, n_dp - 1)),
            dma((2, chunks)),
            dma((chunks,)),
            dma((chunks,)),
            pltpu.SemaphoreType.REGULAR((4,)),
            pltpu.VMEM((chunks, tokens, rows), BF16),
            pltpu.VMEM((tokens, width), BF16),
            dma((-(-width // 256),)),
        ],
        compiler_params=pltpu.CompilerParams(
            collective_id=0, has_side_effects=True, vmem_limit_bytes=60 * 1024 * 1024
        ),
    )(
        routes.T, probs.T, out_grad, gate_pre[0, 0], up_pre[0, 0], gate[0], up[0], down[0].T
    )


def solution(mesh):
    placed = (
        P(("dp", "expert"), "tensor"),
        P(("dp", "expert"), None),
        P(("dp", "expert"), None),
        P("dp", "expert", None, "tensor"),
        P("dp", "expert", None, "tensor"),
        P("expert", None, "tensor"),
        P("expert", None, "tensor"),
        P("expert", "tensor", "dp"),
    )
    return jax.shard_map(
        functools.partial(local, STEPS, NX),
        mesh=mesh,
        in_specs=placed,
        out_specs=P(("dp", "expert"), "tensor"),
        check_vma=False,
    )
```
